32 devices in a mesh: ep: 8 (over z, x), tp: 4 (over y, core).
Axes of the slice: x: 2, y: 2, z: 4, core: 2. Of those that a mesh axis runs over, the one named last changes fastest.
Arguments:
- tokens: bfloat16 [2, 128, 4096], P(None, 'ep'), may hold values from -6 to 6
- route_ids: int32 [2, 128, 8], P(None, 'ep'), may hold values from 0 to 15, all different within a row; in each aligned block of 16 rows (0 to 15, 16 to 31, ..., all dimensions but the last counted through in order) at most 10 rows name the same one
- route_weights: float32 [2, 128, 8], P(None, 'ep'), may hold values from 0.1 to 0.4
- train_map: int32 [64], replicated, may hold values from 0 to 63, each once
- serve_place: int32 [64], replicated, may hold values from 0 to 15, as said below
- train_gate: bfloat16 [64, 1024, 1536], P('ep', None, 'tp'), may hold values from -0.09375 to 0.09375
- train_up: bfloat16 [64, 1024, 1536], P('ep', None, 'tp'), may hold values from -0.09375 to 0.09375
- train_down: bfloat16 [64, 1024, 1536], P('ep', None, 'tp'), may hold values from -0.15625 to 0.15625
Outputs:
- serve_gate: bfloat16 [64, 4096, 1536], P('ep', None, 'tp')
- serve_up: bfloat16 [64, 4096, 1536], P('ep', None, 'tp')
- serve_down: bfloat16 [64, 4096, 1536], P('ep', None, 'tp')
- moe_out: bfloat16 [2, 128, 4096], P(None, 'ep', 'tp')
The draws below stay inside these ranges and needn't reach their ends.
Inputs may be any that keep to these rules, and one draw needn't show every extreme that they name: `route_ids`: each row names 8 different experts; in each aligned block of 16 rows (one index of ep in one step) no expert is named by more than 10 rows. `train_map`: each trainer slot holds a different piece; piece q is part q % 4 of expert q // 4. `serve_place`: every expert occupies two or more serving slots, and some expert exactly two.
All inputs are finite; a program needn't handle non-finite values.
Results may differ from the reference program's by a relative error of at most 0.012.
Values may be sent and summed in bfloat16 or wider, within the bound.
A program may use at most 256 MiB of HBM per device.

```python
import math
import jax
import jax.numpy as jnp
import numpy as np
from jax import lax

D = 4096
FF = 1536
TOPK = 8
EXPERTS = 16
SLOTS = 64
STEPS = 2
TOK_DEV = 16
PARTS_SIZE = 4
QUARTER = 384
TOKENS = 128
MOST = 10
N_EP = 8


def draw_serve_place(key, part):
    key_spare = jax.random.fold_in(key, 101)
    key_first = jax.random.fold_in(key, 202)
    key_second = jax.random.fold_in(key, 303)
    key_shuffle = jax.random.fold_in(key, 404)
    initial = jnp.arange(2 * EXPERTS, dtype=jnp.int32) % EXPERTS
    spare_expert = jax.random.randint(key_spare, (), 0, EXPERTS, dtype=jnp.int32)
    extra_slots = SLOTS - 2 * EXPERTS
    first_factor = jax.random.randint(key_first, (extra_slots,), 0, EXPERTS - 1, dtype=jnp.int32)
    second_factor = jax.random.randint(key_second, (extra_slots,), 0, EXPERTS - 1, dtype=jnp.int32)
    offset = first_factor * second_factor // (EXPERTS - 1)
    extra_experts = (spare_expert + 1 + offset) % EXPERTS
    combined = jnp.concatenate([initial, extra_experts.astype(jnp.int32)])
    shuffle = jax.random.permutation(key_shuffle, SLOTS)
    return combined[shuffle].astype(jnp.int32)


def levels(stream_key, shape, cuts, smallest, high):
    def one(position, shards_of):
        heights = jax.random.uniform(jax.random.fold_in(jax.random.fold_in(stream_key, 6), position), (shards_of,), jnp.float32, smallest / len(cuts), high / len(cuts))
        return jnp.repeat(jnp.exp(heights), shape[position] // shards_of).reshape((-1,) + (1,) * (len(shape) - position - 1))

    loudness = one(*cuts[0])
    for cut in cuts[1:]:
        loudness = loudness * one(*cut)
    return loudness


def assign_block(rng, own, number, rows, count, top, reach, slope):
    ranking = jax.random.permutation(rng, count)
    crowded, common = shares(count, rows * top, reach, slope, True), shares(count, rows * top, reach, slope, False)
    places = jnp.arange(count)

    def named(tallies, rotation):
        used = int((tallies > 0).sum())
        fixed = max(1, used // 4)
        moved = fixed + (places - fixed + rotation * (used - fixed)) % max(1, count - fixed)
        return jnp.zeros((count,), jnp.int32).at[ranking[jnp.where(places < fixed, places, moved)]].set(jnp.asarray(tallies, jnp.int32))

    tallies = jnp.where(number % 4 == 0, named(crowded, number // 4), named(common, number - number // 4 - 1))
    mixed = jax.random.permutation(jax.random.fold_in(own, 3), count)
    donor, taker = mixed[0:count // 2 * 2:2], mixed[1:count // 2 * 2:2]
    slack = jnp.minimum(tallies[donor] - 1, reach - tallies[taker]) // 2
    slack = jnp.where((donor == ranking[0]) | (taker == ranking[0]) | (tallies[taker] == 0), 0, jnp.maximum(slack, 0))
    moved = jax.random.randint(jax.random.fold_in(own, 4), (count // 2,), 0, 1 << 20) % (slack + 1)
    tallies = tallies.at[donor].add(-moved).at[taker].add(moved)
    members = jnp.searchsorted(jnp.cumsum(tallies), jnp.arange(rows * top), side="right").astype(jnp.int32)
    grid = members.reshape(top, rows).T
    grid = grid[jax.random.permutation(jax.random.fold_in(own, 1), rows)]
    rotation = jax.random.randint(jax.random.fold_in(own, 2), (rows, 1), 0, top)
    return jnp.take_along_axis(grid, (jnp.arange(top)[None, :] + rotation) % top, axis=1)


def shares(count, total, bound, lean, full):
    weights = [(1 << 20) // math.isqrt(grade ** lean) + 1 for grade in range(1, count + 1)]
    largest = bound if full else min(bound, max(-(-total // count), total * weights[0] // sum(weights)))
    least = 1 if total - largest >= count - 1 else 0
    given, spare = [largest] + [least] * (count - 1), total - largest - least * (count - 1)
    while spare > 0:
        movable = [i for i in range(1, count) if given[i] < largest] or [i for i in range(1, count) if given[i] < bound]
        pool, budget = sum([weights[i] for i in movable]), spare
        for i in movable:
            more = min(bound - given[i], max(1, budget * weights[i] // pool), spare)
            given[i] = given[i] + more
            spare = spare - more
    return np.array(given)


def scatter_about(own_key, shape, spread, limit, cuts=(), kind=jnp.bfloat16):
    factor_of = levels(own_key, shape, cuts, -0.22, 0.18) if cuts else 1.0
    result = jax.random.normal(own_key, shape, jnp.float32) * spread * factor_of
    return jnp.minimum(jnp.maximum(result, -limit), limit).astype(kind)


def setup_inputs(seed: int = 0) -> dict:
    key_list = jax.random.split(jax.random.key(seed), 9)
    tokens = scatter_about(key_list[0], (STEPS, TOKENS, D), 1.0, 6.0, ((1, 8),))
    route_ids_keys = jax.random.split(jax.random.fold_in(key_list[1], 1), STEPS * TOKENS // TOK_DEV)
    route_ids_turns = jax.random.permutation(jax.random.fold_in(key_list[1], 3), STEPS * TOKENS // TOK_DEV)
    route_ids = jax.vmap(lambda own, number: assign_block(jax.random.fold_in(key_list[1], 2), own, number, TOK_DEV, EXPERTS, TOPK, MOST, 2))(route_ids_keys, route_ids_turns).reshape((STEPS, TOKENS, TOPK))
    route_weights = jnp.clip(0.1 + 0.3 * jax.random.uniform(key_list[2], (STEPS, TOKENS, TOPK), jnp.float32) ** levels(key_list[2], (STEPS, TOKENS, TOPK), ((1, 8),), -0.2, 0.2), 0.1, 0.4)
    train_map = jax.random.permutation(key_list[3], SLOTS).astype(jnp.int32)
    serve_place = draw_serve_place(jax.random.fold_in(key_list[8], 71), 0)
    train_gate = scatter_about(key_list[5], (SLOTS, D // PARTS_SIZE, FF), D ** -0.5, 0.09375, ((0, 8), (2, 4)))
    train_up = scatter_about(key_list[6], (SLOTS, D // PARTS_SIZE, FF), D ** -0.5, 0.09375, ((0, 8), (2, 4)))
    train_down = scatter_about(key_list[7], (SLOTS, D // PARTS_SIZE, FF), FF ** -0.5, 0.15625, ((0, 8), (2, 4)))
    return {"tokens": tokens, "route_ids": route_ids, "route_weights": route_weights, "train_map": train_map, "serve_place": serve_place, "train_gate": train_gate, "train_up": train_up, "train_down": train_down}


def reference(tokens, route_ids, route_weights, train_map, serve_place, train_gate, train_up, train_down):
    inverse = jnp.argsort(train_map).astype(jnp.int32)
    expert_gate = train_gate[inverse].reshape(EXPERTS, D, FF)
    expert_up = train_up[inverse].reshape(EXPERTS, D, FF)
    expert_down = train_down[inverse].reshape(EXPERTS, D, FF)
    place_index = serve_place.astype(jnp.int32)
    serve_gate = expert_gate[place_index]
    serve_up = expert_up[place_index]
    serve_down = expert_down[place_index]
    capacity = min(TOKENS, N_EP * MOST)
    results = []
    for decode_step in range(STEPS):
        pair_experts = route_ids[decode_step].reshape(-1)
        pair_weights = route_weights[decode_step].reshape(-1)
        step_tokens = tokens[decode_step]

        def add_expert(expert, running):
            matches = pair_experts == expert
            ordering = jnp.argsort(jnp.where(matches, 0, 1).astype(jnp.int32), stable=True)[:capacity].astype(jnp.int32)
            valid_pair = matches[ordering]
            token_rows = (ordering // TOPK).astype(jnp.int32)
            inputs = step_tokens[token_rows]
            gate_act = jnp.dot(inputs, expert_gate[expert], preferred_element_type=jnp.float32)
            up_act = jnp.dot(inputs, expert_up[expert], preferred_element_type=jnp.float32)
            hidden = (jax.nn.silu(gate_act) * up_act).astype(jnp.bfloat16)
            down_rows = expert_down[expert]
            summed = jnp.zeros((capacity, D), jnp.float32)
            for quarter_index in range(FF // QUARTER):
                lower = quarter_index * QUARTER
                partial_value = jnp.dot(hidden[:, lower:lower + QUARTER], down_rows[:, lower:lower + QUARTER].T, preferred_element_type=jnp.float32).astype(jnp.bfloat16)
                partial_value = lax.optimization_barrier(partial_value)
                summed = summed + partial_value.astype(jnp.float32)
            expert_out = summed.astype(jnp.bfloat16)
            pair_scale = jnp.where(valid_pair, pair_weights[ordering], jnp.zeros_like(pair_weights[ordering]))
            return running.at[token_rows].add(pair_scale[:, None] * expert_out.astype(jnp.float32))

        running = lax.fori_loop(0, EXPERTS, add_expert, jnp.zeros((TOKENS, D), jnp.float32))
        results.append(running.astype(jnp.bfloat16))
    return serve_gate, serve_up, serve_down, jnp.stack(results)
```

```python
import functools

import jax
import jax.numpy as jnp
from jax import lax
from jax.experimental import pallas as pl
from jax.experimental.pallas import tpu as pltpu
from jax.sharding import PartitionSpec as P

EXPERTS = 16
MOST = 10
MESH = pl.DeviceIdType.MESH


def relay_kernel(
    pairs, chunk_rows, buffers, idx_ref, t0, t1, t2, o0, o1, o2, held, whole, own, other,
    local_sem, first_send, first_recv, line_send, line_recv,
    own_sem, other_send, other_recv, stage_sem, credit_x, credit_up, credit_down,
):
    trains, outs = (t0, t1, t2), (o0, o1, o2)
    me = lax.axis_index("ep")
    z, x = lax.div(me, 2), lax.rem(me, 2)
    partner = me + 1 - 2 * x
    above, below = me + 2, me - 2
    local = t0.shape[0]
    half = t0.shape[1] // 2
    steps = half // chunk_rows
    total = len(trains) * steps
    layer = 2 * local
    picks = own.shape[1]
    recv_slots = other_recv.shape[0]
    has_up, has_down = z < pairs - 1, z > 0

    barrier = pltpu.get_barrier_semaphore()
    pl.semaphore_signal(barrier, inc=1, device_id={"ep": partner}, device_id_type=MESH)

    @pl.when(has_up)
    def _():
        pl.semaphore_signal(barrier, inc=1, device_id={"ep": above}, device_id_type=MESH)

    @pl.when(has_down)
    def _():
        pl.semaphore_signal(barrier, inc=1, device_id={"ep": below}, device_id_type=MESH)

    pl.semaphore_wait(barrier, 1 + jnp.where(has_up, 1, 0) + jnp.where(has_down, 1, 0))

    def rows_of(side, step):
        return pl.ds(pl.multiple_of(side * half + step * chunk_rows, chunk_rows), chunk_rows)

    def mine(slot):
        return held.at[slot, pl.ds(me * local, local)]

    def region(slot, level):
        return held.at[slot, pl.ds(level * layer, layer)]

    def load_copy(train, step, slot):
        return pltpu.make_async_copy(
            train.at[:, rows_of(x, step), :], mine(slot), local_sem.at[slot]
        )

    def first_copy(train, step, slot):
        return pltpu.make_async_remote_copy(
            src_ref=train.at[:, rows_of(1 - x, step), :],
            dst_ref=mine(slot),
            send_sem=first_send.at[slot],
            recv_sem=first_recv.at[slot],
            device_id={"ep": partner},
            device_id_type=MESH,
        )

    def up_copy(slot, level):
        return pltpu.make_async_remote_copy(
            src_ref=region(slot, level),
            dst_ref=region(slot, level),
            send_sem=line_send.at[slot, level],
            recv_sem=line_recv.at[slot, level],
            device_id={"ep": above},
            device_id_type=MESH,
        )

    def down_copy(slot, level):
        return pltpu.make_async_remote_copy(
            src_ref=region(slot, level),
            dst_ref=region(slot, level),
            send_sem=line_send.at[slot, level + 1],
            recv_sem=line_recv.at[slot, level],
            device_id={"ep": below},
            device_id_type=MESH,
        )

    def own_copy(out, step, stage):
        return pltpu.make_async_copy(
            own.at[stage], out.at[:, rows_of(x, step), :], own_sem.at[stage]
        )

    def other_copy(out, step, stage, recv_slot):
        return pltpu.make_async_remote_copy(
            src_ref=other.at[stage],
            dst_ref=out.at[:, rows_of(x, step), :],
            send_sem=other_send.at[stage],
            recv_sem=other_recv.at[recv_slot],
            device_id={"ep": partner},
            device_id_type=MESH,
        )

    def stage_start(n):
        slot = lax.rem(n, buffers)

        @pl.when(n >= buffers)
        def _():
            pl.semaphore_wait(credit_x, 1)

        for a in range(len(trains)):

            @pl.when((n >= a * steps) & (n < (a + 1) * steps))
            def _():
                first_copy(trains[a], n - a * steps, slot).start()
                load_copy(trains[a], n - a * steps, slot).start()

    def stage_send(n):
        slot = lax.rem(n, buffers)
        load_copy(t0, 0, slot).wait()
        first_copy(t0, 0, slot).wait()

        @pl.when(has_up)
        def _():
            @pl.when(n >= buffers)
            def _():
                pl.semaphore_wait(credit_up, 1)

            up_copy(slot, z).start()

        @pl.when(has_down)
        def _():
            @pl.when(n >= buffers)
            def _():
                pl.semaphore_wait(credit_down, 1)

            down_copy(slot, z).start()

    def stage_forward(n, distance):
        slot = lax.rem(n, buffers)

        @pl.when(z - distance >= 0)
        def _():
            up_copy(slot, z - distance).wait_recv()

            @pl.when(has_up)
            def _():
                up_copy(slot, z - distance).start()

        @pl.when(z + distance < pairs)
        def _():
            down_copy(slot, z + distance).wait_recv()

            @pl.when(has_down)
            def _():
                down_copy(slot, z + distance).start()

    def stage_finish(n):
        slot = lax.rem(n, buffers)
        stage = lax.rem(n, 2)
        taken = pltpu.make_async_copy(held.at[slot], whole, stage_sem)
        taken.start()

        def drain_up(level, carry):
            up_copy(slot, level).wait_send()
            return carry

        def drain_down(level, carry):
            down_copy(slot, level).wait_send()
            return carry

        @pl.when(has_up)
        def _():
            lax.fori_loop(0, z + 1, drain_up, 0)

        @pl.when(has_down)
        def _():
            lax.fori_loop(z, pairs, drain_down, 0)

        taken.wait()

        @pl.when(n < total - buffers)
        def _():
            pl.semaphore_signal(credit_x, inc=1, device_id={"ep": partner}, device_id_type=MESH)

            @pl.when(has_up)
            def _():
                pl.semaphore_signal(
                    credit_down, inc=1, device_id={"ep": above}, device_id_type=MESH
                )

            @pl.when(has_down)
            def _():
                pl.semaphore_signal(
                    credit_up, inc=1, device_id={"ep": below}, device_id_type=MESH
                )

        @pl.when(n >= 2)
        def _():
            own_copy(o0, 0, stage).wait()
            other_copy(o0, 0, stage, 0).wait_send()

        @pl.when(n >= 1)
        def _():
            other_copy(o0, 0, stage, lax.rem(n - 1, recv_slots)).wait_recv()

        def pick(s, carry):
            other[stage, s] = whole[idx_ref[picks + s]]
            own[stage, s] = whole[idx_ref[s]]
            return carry

        lax.fori_loop(0, picks, pick, 0)
        for a in range(len(trains)):

            @pl.when((n >= a * steps) & (n < (a + 1) * steps))
            def _():
                other_copy(outs[a], n - a * steps, stage, lax.rem(n, recv_slots)).start()
                own_copy(outs[a], n - a * steps, stage).start()

    def iteration(i, carry):
        @pl.when(i < total)
        def _():
            stage_start(i)

        @pl.when((i >= 1) & (i - 1 < total))
        def _():
            stage_send(i - 1)

        def hop(distance, inner):
            n = i - 1 - distance

            @pl.when((n >= 0) & (n < total))
            def _():
                stage_forward(n, distance)

            return inner

        lax.fori_loop(1, pairs, hop, 0)

        @pl.when(i >= pairs)
        def _():
            stage_finish(i - pairs)

        return carry

    lax.fori_loop(0, total + pairs, iteration, 0)
    for n in range(max(total - 2, 0), total):
        own_copy(o0, 0, n % 2).wait()
        other_copy(o0, 0, n % 2, 0).wait_send()
    other_copy(o0, 0, 0, (total - 1) % recv_slots).wait_recv()


def relay(idx, trains, ep_count, part_count):
    local, piece_rows, width = trains[0].shape
    pairs = ep_count // 2
    slots = ep_count * local
    buffers = pairs + 3
    chunk_rows = 32
    while chunk_rows > 16 and buffers * slots * chunk_rows * width * 2 > 24 * 2**20:
        chunk_rows //= 2
    picks = local * part_count
    dma = pltpu.SemaphoreType.DMA
    any_spec = pl.BlockSpec(memory_space=pl.ANY)
    return pl.pallas_call(
        functools.partial(relay_kernel, pairs, chunk_rows, buffers),
        out_shape=[jax.ShapeDtypeStruct((picks, piece_rows, width), jnp.bfloat16)] * 3,
        in_specs=[pl.BlockSpec(memory_space=pltpu.SMEM)] + [any_spec] * 3,
        out_specs=[any_spec] * 3,
        scratch_shapes=[
            pltpu.VMEM((buffers, slots, chunk_rows, width), jnp.bfloat16),
            pltpu.VMEM((slots, chunk_rows, width), jnp.bfloat16),
            pltpu.VMEM((2, picks, chunk_rows, width), jnp.bfloat16),
            pltpu.VMEM((2, picks, chunk_rows, width), jnp.bfloat16),
            dma((buffers,)),
            dma((buffers,)),
            dma((buffers,)),
            dma((buffers, pairs + 1)),
            dma((buffers, pairs)),
            dma((2,)),
            dma((2,)),
            dma((buffers + 2,)),
            dma,
            pltpu.SemaphoreType.REGULAR,
            pltpu.SemaphoreType.REGULAR,
            pltpu.SemaphoreType.REGULAR,
        ],
        compiler_params=pltpu.CompilerParams(
            collective_id=0, has_side_effects=True, vmem_limit_bytes=56 * 2**20
        ),
    )(idx, *trains)


def body(
    tokens, route_ids, route_weights, train_map, serve_place, train_gate, train_up, train_down
):
    ep_count = lax.axis_size("ep")
    tp_count = lax.axis_size("tp")
    ep_index = lax.axis_index("ep")
    slot_count = serve_place.shape[0]
    local_slots, piece_rows, quarter_width = train_gate.shape
    part_count = slot_count // EXPERTS
    slot_iota = jnp.arange(slot_count, dtype=jnp.int32)
    inverse = jnp.sum(
        jnp.where(train_map[:, None] == slot_iota[None, :], slot_iota[:, None], 0), axis=0
    )
    wanted = (
        serve_place[:, None] * part_count + jnp.arange(part_count, dtype=jnp.int32)[None, :]
    ).reshape(-1)
    source_slot = jnp.sum(
        jnp.where(wanted[:, None] == slot_iota[None, :], inverse[None, :], 0), axis=1
    ).reshape(ep_count, local_slots * part_count)
    partner = ep_index + 1 - 2 * (ep_index % 2)
    idx = jnp.concatenate(
        [
            lax.dynamic_index_in_dim(source_slot, ep_index, 0, keepdims=False),
            lax.dynamic_index_in_dim(source_slot, partner, 0, keepdims=False),
        ]
    ).astype(jnp.int32)
    model_rows = part_count * piece_rows
    serve_gate, serve_up, serve_down = (
        o.reshape(local_slots, model_rows, quarter_width)
        for o in relay(idx, (train_gate, train_up, train_down), ep_count, part_count)
    )

    step_count, tok_count, model_width = tokens.shape
    topk_count = route_ids.shape[2]
    pair_count = tok_count * topk_count
    capacity = (MOST + 1) // 2
    buffer_rows = slot_count * capacity
    out_width = model_width // tp_count
    same_slot = serve_place[:, None] == serve_place[None, :]
    replica_rank = jnp.sum(same_slot & (slot_iota[None, :] < slot_iota[:, None]), axis=1)
    pair_iota = jnp.arange(pair_count, dtype=jnp.int32)

    def place(ids):
        pair_experts = ids.reshape(pair_count)
        holders = serve_place[None, :] == pair_experts[:, None]
        replica_count = jnp.sum(holders, axis=1)
        earlier_pairs = (pair_experts[:, None] == pair_experts[None, :]) & (
            pair_iota[None, :] < pair_iota[:, None]
        )
        seen = jnp.sum(earlier_pairs, axis=1)
        target = (seen + ep_index) % replica_count
        position = seen // replica_count
        chosen = holders & (replica_rank[None, :] == target[:, None])
        dest_slot = jnp.sum(jnp.where(chosen, slot_iota[None, :], 0), axis=1)
        row_index = dest_slot * capacity + position
        placing = row_index[None, :] == jnp.arange(buffer_rows, dtype=jnp.int32)[:, None]
        return placing.reshape(buffer_rows, tok_count, topk_count)

    placing = jax.vmap(place)(route_ids)
    send_rows = jnp.einsum(
        "tbi,tid->btd",
        jnp.any(placing, axis=3).astype(jnp.bfloat16),
        tokens,
        preferred_element_type=jnp.float32,
    ).astype(jnp.bfloat16)
    send_rows = send_rows.reshape(ep_count, local_slots, capacity * step_count, model_width)
    received = lax.all_to_all(send_rows, "ep", split_axis=0, concat_axis=0, tiled=True)
    received = received.transpose(1, 0, 2, 3).reshape(
        local_slots, ep_count * capacity * step_count, model_width
    )
    gate_act = jnp.einsum("lmd,ldf->lmf", received, serve_gate, preferred_element_type=jnp.float32)
    up_act = jnp.einsum("lmd,ldf->lmf", received, serve_up, preferred_element_type=jnp.float32)
    hidden = (jax.nn.silu(gate_act) * up_act).astype(jnp.bfloat16)
    partial_value = jnp.einsum(
        "lmf,ldf->lmd", hidden, serve_down, preferred_element_type=jnp.float32
    ).astype(jnp.bfloat16)
    partial_value = lax.optimization_barrier(partial_value)
    summed = lax.psum_scatter(partial_value, "tp", scatter_dimension=2, tiled=True)
    summed = summed.reshape(
        local_slots, ep_count, capacity * step_count, out_width
    ).transpose(1, 0, 2, 3)
    returned = lax.all_to_all(summed, "ep", split_axis=0, concat_axis=0, tiled=True)
    flat_out = returned.reshape(buffer_rows, step_count, out_width)
    mixing = jnp.sum(jnp.where(placing, route_weights[:, None], 0.0), axis=3)
    moe_out = jnp.einsum(
        "tbi,btd->tid",
        mixing,
        flat_out.astype(jnp.float32),
        precision=lax.Precision.HIGHEST,
        preferred_element_type=jnp.float32,
    ).astype(jnp.bfloat16)
    return (serve_gate, serve_up, serve_down, moe_out)


def solution(mesh):
    in_specs = (
        P(None, "ep", None),
        P(None, "ep", None),
        P(None, "ep", None),
        P(),
        P(),
        P("ep", None, "tp"),
        P("ep", None, "tp"),
        P("ep", None, "tp"),
    )
    out_specs = (P("ep", None, "tp"), P("ep", None, "tp"), P("ep", None, "tp"), P(None, "ep", "tp"))
    return jax.shard_map(body, mesh=mesh, in_specs=in_specs, out_specs=out_specs, check_vma=False)
```

```python
import functools

import jax
import jax.numpy as jnp
from jax import lax
from jax.experimental import pallas as pl
from jax.experimental.pallas import tpu as pltpu
from jax.sharding import PartitionSpec as P

EXPERTS = 16
MOST = 10
MESH = pl.DeviceIdType.MESH


def relay_kernel(
    pairs, chunk_rows, buffers, idx_ref, t0, t1, t2, o0, o1, o2, held, whole, own, other,
    local_sem, first_send, first_recv, line_send, line_recv,
    own_sem, other_send, other_recv, stage_sem, credit_x, credit_up, credit_down,
):
    trains, outs = (t0, t1, t2), (o0, o1, o2)
    me = lax.axis_index("ep")
    z, x = lax.div(me, 2), lax.rem(me, 2)
    partner = me + 1 - 2 * x
    above, below = me + 2, me - 2
    local = t0.shape[0]
    half = t0.shape[1] // 2
    steps = half // chunk_rows
    total = len(trains) * steps
    layer = 2 * local
    picks = own.shape[1]
    recv_slots = other_recv.shape[0]
    has_up, has_down = z < pairs - 1, z > 0

    barrier = pltpu.get_barrier_semaphore()
    pl.semaphore_signal(barrier, inc=1, device_id={"ep": partner}, device_id_type=MESH)

    @pl.when(has_up)
    def _():
        pl.semaphore_signal(barrier, inc=1, device_id={"ep": above}, device_id_type=MESH)

    @pl.when(has_down)
    def _():
        pl.semaphore_signal(barrier, inc=1, device_id={"ep": below}, device_id_type=MESH)

    pl.semaphore_wait(barrier, 1 + jnp.where(has_up, 1, 0) + jnp.where(has_down, 1, 0))

    def rows_of(side, step):
        return pl.ds(pl.multiple_of(side * half + step * chunk_rows, chunk_rows), chunk_rows)

    def mine(slot):
        return held.at[slot, pl.ds(me * local, local)]

    def region(slot, level):
        return held.at[slot, pl.ds(level * layer, layer)]

    def load_copy(train, step, slot):
        return pltpu.make_async_copy(
            train.at[:, rows_of(x, step), :], mine(slot), local_sem.at[slot]
        )

    def first_copy(train, step, slot):
        return pltpu.make_async_remote_copy(
            src_ref=train.at[:, rows_of(1 - x, step), :],
            dst_ref=mine(slot),
            send_sem=first_send.at[slot],
            recv_sem=first_recv.at[slot],
            device_id={"ep": partner},
            device_id_type=MESH,
        )

    def up_copy(slot, level):
        return pltpu.make_async_remote_copy(
            src_ref=region(slot, level),
            dst_ref=region(slot, level),
            send_sem=line_send.at[slot, level],
            recv_sem=line_recv.at[slot, level],
            device_id={"ep": above},
            device_id_type=MESH,
        )

    def down_copy(slot, level):
        return pltpu.make_async_remote_copy(
            src_ref=region(slot, level),
            dst_ref=region(slot, level),
            send_sem=line_send.at[slot, level + 1],
            recv_sem=line_recv.at[slot, level],
            device_id={"ep": below},
            device_id_type=MESH,
        )

    def own_copy(out, step, stage):
        return pltpu.make_async_copy(
            own.at[stage], out.at[:, rows_of(x, step), :], own_sem.at[stage]
        )

    def other_copy(out, step, stage, recv_slot):
        return pltpu.make_async_remote_copy(
            src_ref=other.at[stage],
            dst_ref=out.at[:, rows_of(x, step), :],
            send_sem=other_send.at[stage],
            recv_sem=other_recv.at[recv_slot],
            device_id={"ep": partner},
            device_id_type=MESH,
        )

    def stage_start(n):
        slot = lax.rem(n, buffers)

        @pl.when(n >= buffers)
        def _():
            pl.semaphore_wait(credit_x, 1)

        for a in range(len(trains)):

            @pl.when((n >= a * steps) & (n < (a + 1) * steps))
            def _():
                first_copy(trains[a], n - a * steps, slot).start()
                load_copy(trains[a], n - a * steps, slot).start()

    def stage_send(n):
        slot = lax.rem(n, buffers)
        load_copy(t0, 0, slot).wait()
        first_copy(t0, 0, slot).wait()

        @pl.when(has_up)
        def _():
            @pl.when(n >= buffers)
            def _():
                pl.semaphore_wait(credit_up, 1)

            up_copy(slot, z).start()

        @pl.when(has_down)
        def _():
            @pl.when(n >= buffers)
            def _():
                pl.semaphore_wait(credit_down, 1)

            down_copy(slot, z).start()

    def stage_forward(n, distance):
        slot = lax.rem(n, buffers)

        @pl.when(z - distance >= 0)
        def _():
            up_copy(slot, z - distance).wait_recv()

            @pl.when(has_up)
            def _():
                up_copy(slot, z - distance).start()

        @pl.when(z + distance < pairs)
        def _():
            down_copy(slot, z + distance).wait_recv()

            @pl.when(has_down)
            def _():
                down_copy(slot, z + distance).start()

    def stage_finish(n):
        slot = lax.rem(n, buffers)
        stage = lax.rem(n, 2)
        taken = pltpu.make_async_copy(held.at[slot], whole, stage_sem)
        taken.start()

        def drain_up(level, carry):
            up_copy(slot, level).wait_send()
            return carry

        def drain_down(level, carry):
            down_copy(slot, level).wait_send()
            return carry

        @pl.when(has_up)
        def _():
            lax.fori_loop(0, z + 1, drain_up, 0)

        @pl.when(has_down)
        def _():
            lax.fori_loop(z, pairs, drain_down, 0)

        taken.wait()

        @pl.when(n < total - buffers)
        def _():
            pl.semaphore_signal(credit_x, inc=1, device_id={"ep": partner}, device_id_type=MESH)

            @pl.when(has_up)
            def _():
                pl.semaphore_signal(
                    credit_down, inc=1, device_id={"ep": above}, device_id_type=MESH
                )

            @pl.when(has_down)
            def _():
                pl.semaphore_signal(
                    credit_up, inc=1, device_id={"ep": below}, device_id_type=MESH
                )

        @pl.when(n >= 2)
        def _():
            own_copy(o0, 0, stage).wait()
            other_copy(o0, 0, stage, 0).wait_send()

        @pl.when(n >= 1)
        def _():
            other_copy(o0, 0, stage, lax.rem(n - 1, recv_slots)).wait_recv()

        def pick(s, carry):
            other[stage, s] = whole[idx_ref[picks + s]]
            own[stage, s] = whole[idx_ref[s]]
            return carry

        lax.fori_loop(0, picks, pick, 0)
        for a in range(len(trains)):

            @pl.when((n >= a * steps) & (n < (a + 1) * steps))
            def _():
                other_copy(outs[a], n - a * steps, stage, lax.rem(n, recv_slots)).start()
                own_copy(outs[a], n - a * steps, stage).start()

    def iteration(i, carry):
        @pl.when(i < total)
        def _():
            stage_start(i)

        @pl.when((i >= 1) & (i - 1 < total))
        def _():
            stage_send(i - 1)

        def hop(distance, inner):
            n = i - 1 - distance

            @pl.when((n >= 0) & (n < total))
            def _():
                stage_forward(n, distance)

            return inner

        lax.fori_loop(1, pairs, hop, 0)

        @pl.when(i >= pairs)
        def _():
            stage_finish(i - pairs)

        return carry

    lax.fori_loop(0, total + pairs, iteration, 0)
    for n in range(max(total - 2, 0), total):
        own_copy(o0, 0, n % 2).wait()
        other_copy(o0, 0, n % 2, 0).wait_send()
    other_copy(o0, 0, 0, (total - 1) % recv_slots).wait_recv()


def relay(idx, trains, ep_count, part_count):
    local, piece_rows, width = trains[0].shape
    pairs = ep_count // 2
    slots = ep_count * local
    buffers = pairs + 3
    chunk_rows = 32
    while chunk_rows > 16 and buffers * slots * chunk_rows * width * 2 > 24 * 2**20:
        chunk_rows //= 2
    picks = local * part_count
    dma = pltpu.SemaphoreType.DMA
    any_spec = pl.BlockSpec(memory_space=pl.ANY)
    return pl.pallas_call(
        functools.partial(relay_kernel, pairs, chunk_rows, buffers),
        out_shape=[jax.ShapeDtypeStruct((picks, piece_rows, width), jnp.bfloat16)] * 3,
        in_specs=[pl.BlockSpec(memory_space=pltpu.SMEM)] + [any_spec] * 3,
        out_specs=[any_spec] * 3,
        scratch_shapes=[
            pltpu.VMEM((buffers, slots, chunk_rows, width), jnp.bfloat16),
            pltpu.VMEM((slots, chunk_rows, width), jnp.bfloat16),
            pltpu.VMEM((2, picks, chunk_rows, width), jnp.bfloat16),
            pltpu.VMEM((2, picks, chunk_rows, width), jnp.bfloat16),
            dma((buffers,)),
            dma((buffers,)),
            dma((buffers,)),
            dma((buffers, pairs + 1)),
            dma((buffers, pairs)),
            dma((2,)),
            dma((2,)),
            dma((buffers + 2,)),
            dma,
            pltpu.SemaphoreType.REGULAR,
            pltpu.SemaphoreType.REGULAR,
            pltpu.SemaphoreType.REGULAR,
        ],
        compiler_params=pltpu.CompilerParams(
            collective_id=0, has_side_effects=True, vmem_limit_bytes=56 * 2**20
        ),
    )(idx, *trains)


def body(
    tokens, route_ids, route_weights, train_map, serve_place, train_gate, train_up, train_down
):
    ep_count = lax.axis_size("ep")
    tp_count = lax.axis_size("tp")
    ep_index = lax.axis_index("ep")
    slot_count = serve_place.shape[0]
    local_slots, piece_rows, quarter_width = train_gate.shape
    part_count = slot_count // EXPERTS
    slot_iota = jnp.arange(slot_count, dtype=jnp.int32)
    inverse = jnp.sum(
        jnp.where(train_map[:, None] == slot_iota[None, :], slot_iota[:, None], 0), axis=0
    )
    wanted = (
        serve_place[:, None] * part_count + jnp.arange(part_count, dtype=jnp.int32)[None, :]
    ).reshape(-1)
    source_slot = jnp.sum(
        jnp.where(wanted[:, None] == slot_iota[None, :], inverse[None, :], 0), axis=1
    ).reshape(ep_count, local_slots * part_count)
    partner = ep_index + 1 - 2 * (ep_index % 2)
    idx = jnp.concatenate(
        [
            lax.dynamic_index_in_dim(source_slot, ep_index, 0, keepdims=False),
            lax.dynamic_index_in_dim(source_slot, partner, 0, keepdims=False),
        ]
    ).astype(jnp.int32)
    model_rows = part_count * piece_rows
    raw_gate, raw_up, raw_down = (
        o.reshape(local_slots, model_rows, quarter_width)
        for o in relay(idx, (train_gate, train_up, train_down), ep_count, part_count)
    )

    step_count, tok_count, model_width = tokens.shape
    topk_count = route_ids.shape[2]
    capacity = (MOST + 1) // 2
    depth = capacity * step_count
    peer_rows = depth * local_slots
    all_tokens = step_count * tok_count
    same_slot = serve_place[:, None] == serve_place[None, :]
    replica_rank = jnp.sum(same_slot & (slot_iota[None, :] < slot_iota[:, None]), axis=1)
    pair_count = tok_count * topk_count
    pair_iota = jnp.arange(pair_count, dtype=jnp.int32)

    def rows(ids, decode_step):
        pair_experts = ids.reshape(pair_count)
        holders = serve_place[None, :] == pair_experts[:, None]
        replica_count = jnp.sum(holders, axis=1)
        earlier_pairs = (pair_experts[:, None] == pair_experts[None, :]) & (
            pair_iota[None, :] < pair_iota[:, None]
        )
        seen = jnp.sum(earlier_pairs, axis=1)
        target = (seen + ep_index) % replica_count
        position = seen // replica_count
        chosen = holders & (replica_rank[None, :] == target[:, None])
        dest_slot = jnp.sum(jnp.where(chosen, slot_iota[None, :], 0), axis=1)
        return (
            dest_slot // local_slots * peer_rows
            + (decode_step * capacity + position) * local_slots
            + dest_slot % local_slots
        )

    row_index = jax.vmap(rows)(route_ids, jnp.arange(step_count, dtype=jnp.int32))
    row_index = row_index.reshape(1, all_tokens, topk_count)
    buffer_iota = jnp.arange(ep_count * peer_rows, dtype=jnp.int32)
    placing = row_index == buffer_iota[:, None, None]
    mixing = jnp.sum(
        jnp.where(placing, route_weights.reshape(1, all_tokens, topk_count), 0.0), axis=2
    )
    send_rows = jnp.dot(
        jnp.any(placing, axis=2).astype(jnp.bfloat16),
        tokens.reshape(all_tokens, model_width),
        preferred_element_type=jnp.float32,
    ).astype(jnp.bfloat16)
    received = lax.all_to_all(
        send_rows.reshape(ep_count, depth, local_slots, model_width),
        "ep", split_axis=0, concat_axis=0, tiled=True,
    ).reshape(ep_count * depth, local_slots, model_width)
    mix = lax.all_to_all(
        mixing.reshape(ep_count, peer_rows, all_tokens),
        "ep", split_axis=0, concat_axis=0, tiled=True,
    )
    gate_act = jnp.einsum("mld,ldf->lmf", received, raw_gate, preferred_element_type=jnp.float32)
    up_act = jnp.einsum("mld,ldf->lmf", received, raw_up, preferred_element_type=jnp.float32)
    hidden = (jax.nn.silu(gate_act) * up_act).astype(jnp.bfloat16)
    partial_value = jnp.einsum(
        "lmf,ldf->lmd", hidden, raw_down, preferred_element_type=jnp.float32
    ).astype(jnp.bfloat16)
    mix = mix.reshape(ep_count, depth, local_slots, all_tokens)
    mix_high = mix.astype(jnp.bfloat16)
    mix_low = (mix - mix_high.astype(jnp.float32)).astype(jnp.bfloat16)
    rows_out = partial_value.reshape(local_slots, ep_count, depth, model_width)

    def combine(part):
        return jnp.einsum("pclt,lpcd->ptd", part, rows_out, preferred_element_type=jnp.float32)

    combined = (combine(mix_high) + combine(mix_low)).astype(jnp.bfloat16)
    combined = lax.optimization_barrier(combined)
    summed = lax.psum_scatter(combined, "tp", scatter_dimension=2, tiled=True)
    raw_gate, raw_up, raw_down, _ = lax.optimization_barrier(
        (raw_gate, raw_up, raw_down, combined)
    )
    serve_gate, serve_up, serve_down = (settle(o) for o in (raw_gate, raw_up, raw_down))
    summed, serve_gate, serve_up = lax.optimization_barrier((summed, serve_gate, serve_up))
    returned = lax.all_to_all(summed, "ep", split_axis=0, concat_axis=0, tiled=True)
    moe_out = jnp.sum(returned.astype(jnp.float32), axis=0).astype(jnp.bfloat16)
    moe_out = moe_out.reshape(step_count, tok_count, model_width // tp_count)
    return (serve_gate, serve_up, serve_down, moe_out)


def settle_kernel(source, target):
    target[...] = source[...]


def settle(source):
    slots, rows, width = source.shape
    spec = pl.BlockSpec((1, rows, width), lambda i: (i, 0, 0))
    return pl.pallas_call(
        settle_kernel,
        grid=(slots,),
        out_shape=jax.ShapeDtypeStruct(source.shape, source.dtype),
        in_specs=[spec],
        out_specs=spec,
        cost_estimate=pl.CostEstimate(
            flops=0, bytes_accessed=4 * slots * rows * width, transcendentals=0
        ),
    )(source)


def solution(mesh):
    in_specs = (
        P(None, "ep", None),
        P(None, "ep", None),
        P(None, "ep", None),
        P(),
        P(),
        P("ep", None, "tp"),
        P("ep", None, "tp"),
        P("ep", None, "tp"),
    )
    out_specs = (P("ep", None, "tp"), P("ep", None, "tp"), P("ep", None, "tp"), P(None, "ep", "tp"))
    return jax.shard_map(body, mesh=mesh, in_specs=in_specs, out_specs=out_specs, check_vma=False)
```
